32 devices in a mesh: dp: 16 (over z, y, x), section: 2 (over core).
Axes of the slice: x: 2, y: 2, z: 4, core: 2. Of those that a mesh axis runs over, the one named last changes fastest.
Arguments:
- section_inputs: bfloat16 [2, 2, 2048, 2048], P('section', None, 'dp'), may hold values from -6 to 6
- mix_weight: bfloat16 [2, 2048, 2048], P('section'), may hold values from -0.0625 to 0.0625
- norm_gain: float32 [2, 2048], P('section'), may hold values from 0.5 to 1.5
- out_cotangent: bfloat16 [2, 2048, 2048], P(None, 'dp'), may hold values from -6 to 6
- positions: int32 [2, 2048], P(None, 'dp'), may hold values from 0 to 1023
Outputs:
- grad_inputs: bfloat16 [2, 2, 2048, 2048], P('section', None, 'dp')
- grad_weight: float32 [2, 2048, 2048], P('section', 'dp')
- grad_gain: float32 [2, 2048], P('section', 'dp')
The draws below stay inside these ranges and needn't reach their ends.
Inputs may be any that keep to these rules, and one draw needn't show every extreme that they name: `positions`: depth index of a token within its tile.
All inputs are finite; a program needn't handle non-finite values.
Results may differ from the reference program's by a relative error of at most 0.017.
Values may be sent and summed in bfloat16 or wider, within the bound.
A program may use at most 128 MiB of HBM per device.

```python
import math
import jax
import jax.numpy as jnp
from jax import lax

CHANNELS = 2048
MICROBATCH = 2
TOKENS_MB = 128
DEPTH = 1024
SECTIONS = 2
TOKENS = 2048
N_DP = 16


def place_ends(drawn, rng, low, high):
    longest = drawn.shape.index(max(drawn.shape))
    spots = []
    for shift in (0, 1):
        where = [jax.random.randint(jax.random.fold_in(rng, axis), (), 0, length) for axis, length in enumerate(drawn.shape)]
        where[longest] = (where[longest] + shift) % drawn.shape[longest]
        spots.append(tuple(where))
    return drawn.at[spots[0]].set(low).at[spots[1]].set(high)


def spiked(values, own_key, source, target, shards_of, factor):
    def block_of(axis_at):
        return (jnp.arange(values.shape[axis_at]) // (values.shape[axis_at] // shards_of)).reshape((-1,) + (1,) * (values.ndim - 1 - axis_at))

    near = jax.random.permutation(own_key, shards_of)[block_of(target)]
    far = (block_of(target) + shards_of // 2) % shards_of
    return jnp.where((block_of(source) == near) | (block_of(source) == far), factor * values, values)


def block_scale(own_key, extent, split, low, largest):
    level, own = 1.0, jax.random.fold_in(own_key, 6)
    for axis_at, shards_of in split:
        draws = jnp.exp(jax.random.uniform(jax.random.fold_in(own, axis_at), (shards_of,), jnp.float32, low / len(split), largest / len(split)))
        level = level * jnp.repeat(draws, extent[axis_at] // shards_of).reshape([-1 if axis == axis_at else 1 for axis in range(len(extent))])
    return level


def centred(rng, shape, spread, limit, shards=(), dtype=jnp.bfloat16):
    array = spread * jax.random.normal(rng, shape, jnp.float32)
    if shards:
        array = array * block_scale(rng, shape, shards, -0.22, 0.18)
    return jnp.clip(array, -limit, limit).astype(dtype)


def heavy_noise(stream_key, dims, deviation, bound, pieces, heavy, dtype=jnp.bfloat16):
    entries = deviation * jax.random.normal(stream_key, dims, jnp.float32)
    if pieces:
        entries = entries * block_scale(stream_key, dims, pieces, -0.22, 0.18)
    return jnp.clip(spiked(entries, jax.random.fold_in(stream_key, 3), *heavy), -bound, bound).astype(dtype)


def setup_inputs(seed: int = 0) -> dict:
    streams_of = jax.random.split(jax.random.key(seed), 6)
    section_inputs = heavy_noise(streams_of[0], (SECTIONS, MICROBATCH, TOKENS, CHANNELS), 1.0, 6.0, ((0, 2), (2, 16)), (2, 3, 16, 2.0))
    mix_weight = centred(streams_of[1], (SECTIONS, CHANNELS, CHANNELS), (4 * CHANNELS) ** -0.5, 0.0625, ((0, 2),))
    norm_gain = jnp.clip(1.0 + 0.1 * jax.random.normal(streams_of[2], (SECTIONS, CHANNELS), jnp.float32), 0.5, 1.5)
    out_cotangent = centred(streams_of[3], (MICROBATCH, TOKENS, CHANNELS), 1.0, 6.0, ((1, 16),))
    positions = place_ends(jax.random.randint(streams_of[4], (MICROBATCH, TOKENS), 0, DEPTH), jax.random.fold_in(streams_of[4], 1), 0, DEPTH - 1).astype(jnp.int32)
    return dict(section_inputs=section_inputs, mix_weight=mix_weight, norm_gain=norm_gain, out_cotangent=out_cotangent, positions=positions)


def section_back(inputs, grad_out, factor, gain_vec, weight_mat):
    inputs_f = inputs.astype(jnp.float32)
    inv_rms = lax.rsqrt(lax.optimization_barrier(jnp.mean(inputs_f * inputs_f, axis=-1, keepdims=True)) + 1e-06)
    normed = inputs_f * inv_rms * gain_vec
    activation, gelu_back = jax.vjp(jax.nn.gelu, normed)
    upstream = (factor[:, None] * grad_out.astype(jnp.float32)).astype(jnp.bfloat16)
    back = lax.dot_general(upstream, weight_mat, (((1,), (1,)), ((), ())), preferred_element_type=jnp.float32)
    grad_norm = gelu_back(back)[0]
    scaled = grad_norm * gain_vec
    projected = lax.optimization_barrier(jnp.mean(scaled * inputs_f, axis=-1, keepdims=True))
    delta = inv_rms * scaled - inputs_f * (inv_rms * inv_rms * inv_rms) * projected
    grad_in = (grad_out.astype(jnp.float32) + delta).astype(jnp.bfloat16)
    gain_term = lax.optimization_barrier(jnp.sum(grad_norm * inputs_f * inv_rms, axis=0))
    return (grad_in, upstream, activation.astype(jnp.bfloat16), gain_term)

def weight_sum(activation, upstream):
    act_blocks = activation.reshape(MICROBATCH * N_DP, TOKENS_MB, CHANNELS)
    up_blocks = upstream.reshape(MICROBATCH * N_DP, TOKENS_MB, CHANNELS)

    def add_block(carry, pair):
        term = lax.dot_general(pair[0], pair[1], (((0,), (0,)), ((), ())), preferred_element_type=jnp.float32)
        rounded = lax.optimization_barrier(term.astype(jnp.bfloat16))
        return (carry + rounded.astype(jnp.float32), None)
    total, _ = lax.scan(add_block, jnp.zeros((CHANNELS, CHANNELS), jnp.float32), (act_blocks, up_blocks))
    return total

def reference(section_inputs, mix_weight, norm_gain, out_cotangent, positions):
    total = MICROBATCH * TOKENS
    depth_gain = 1.0 + 0.5 * jnp.sin(2.0 * math.pi * positions.reshape(total).astype(jnp.float32) / DEPTH)
    grad_out = out_cotangent.reshape(total, CHANNELS)
    grads = []
    weights = []
    gains = []
    for section_idx in range(SECTIONS - 1, -1, -1):
        inputs = section_inputs[section_idx].reshape(total, CHANNELS)
        grad_in, upstream, activation, gain_term = section_back(inputs, grad_out, depth_gain, norm_gain[section_idx], mix_weight[section_idx])
        weights.append(weight_sum(activation, upstream))
        gains.append(gain_term)
        grads.append(grad_in.reshape(MICROBATCH, TOKENS, CHANNELS))
        grad_out = grad_in
    grads = grads[::-1]
    weights = weights[::-1]
    gains = gains[::-1]
    return (jnp.stack(grads), jnp.stack(weights), jnp.stack(gains))
```

```python
import functools
import math

import jax
import jax.numpy as jnp
from jax import lax
from jax.experimental import pallas as pl
from jax.experimental.pallas import tpu as pltpu
from jax.sharding import PartitionSpec as P

DEPTH = 1024
MESH = pl.DeviceIdType.MESH
F32 = jnp.float32
BF16 = jnp.bfloat16


def outer_sum(a, b):
    return lax.dot_general(a, b, (((0,), (0,)), ((), ())), preferred_element_type=F32)


def weight_kernel(
    planes, act_ref, up_ref, gain_ref, out_ref, gain_out,
    gath_a, gath_u, part, from_left, from_right, to_right, to_left, swap_out, swap_in,
    gain_in, gain_mid, gain_sum, gain_z,
    xy_send, xy_recv, r_send, r_recv, l_send, l_recv, g_send, g_recv,
):
    me = lax.axis_index("dp")
    total = planes * 4
    x = lax.rem(me, 2)
    y = lax.rem(me // 2, 2)
    z = me // 4
    xn = me + 1 - 2 * x
    yn = me + 2 - 4 * y
    half = act_ref.shape[2]
    rows = half // planes
    share = rows // 2

    def copy(src, dst, send, recv, to):
        return pltpu.make_async_remote_copy(
            src_ref=src, dst_ref=dst, send_sem=send, recv_sem=recv,
            device_id={"dp": to}, device_id_type=MESH,
        )

    barrier = pltpu.get_barrier_semaphore()
    z_peers = [lax.rem(me + 4 * step, total) for step in range(1, planes)]
    for peer in [xn, yn] + z_peers:
        pl.semaphore_signal(barrier, inc=1, device_id={"dp": peer}, device_id_type=MESH)
    pl.semaphore_wait(barrier, 1 + planes)

    gain_x = copy(gain_ref, gain_in.at[0], g_send.at[0], g_recv.at[0], xn)
    act_x = copy(act_ref.at[1 - x], gath_a.at[0], xy_send.at[0], xy_recv.at[0], xn)
    up_y = copy(up_ref.at[1 - y], gath_u.at[1], xy_send.at[1], xy_recv.at[1], yn)
    up_x = copy(up_ref.at[y], gath_u.at[0], xy_send.at[2], xy_recv.at[2], xn)
    act_y = copy(act_ref.at[x], gath_a.at[1], xy_send.at[3], xy_recv.at[3], yn)
    act_d = copy(gath_a.at[0], gath_a.at[2], xy_send.at[4], xy_recv.at[4], yn)
    up_d = copy(gath_u.at[1], gath_u.at[2], xy_send.at[5], xy_recv.at[5], xn)
    gain_y = copy(gain_mid, gain_in.at[1], g_send.at[1], g_recv.at[1], yn)

    for first in (gain_x, act_x, up_y, up_x, act_y):
        first.start()

    @pl.loop(0, planes)
    def _(b):
        cols = pl.ds(pl.multiple_of(b * rows, 128), rows)
        part[b] = outer_sum(act_ref[x, :, cols], up_ref[y])

    gain_x.wait_recv()
    gain_mid[...] = gain_ref[...] + gain_in[0]
    act_x.wait_recv()
    act_d.start()
    up_y.wait_recv()
    up_d.start()
    gain_y.start()

    def add_source(slot):
        @pl.loop(0, planes)
        def _(b):
            cols = pl.ds(pl.multiple_of(b * rows, 128), rows)
            part[b] += outer_sum(gath_a[slot, :, cols], gath_u[slot])

    up_x.wait_recv()
    add_source(0)
    act_y.wait_recv()
    add_source(1)
    gain_y.wait_recv()
    gain_sum[...] = gain_mid[...] + gain_in[1]
    gain_zs = [
        copy(gain_sum, gain_z.at[step], g_send.at[2 + step], g_recv.at[2 + step], z_peers[step])
        for step in range(planes - 1)
    ]
    for tiny in gain_zs:
        tiny.start()
    act_d.wait_recv()
    up_d.wait_recv()
    add_source(2)

    z_next = lax.rem(me + 4, total)
    z_prev = lax.rem(me + total - 4, total)

    def right(b):
        return copy(to_right.at[b], from_left.at[b], r_send.at[b], r_recv.at[b], z_next)

    def left(b):
        return copy(to_left.at[b], from_right.at[b], l_send.at[b], l_recv.at[b], z_prev)

    for t in range(planes - 1):
        @pl.when(t >= z)
        def _():
            b = planes - 1 - t + z

            @pl.when(z > 0)
            def _():
                right(b).wait_recv()
                to_right[b] = (part[b] + from_left[b].astype(F32)).astype(BF16)

            @pl.when(z == 0)
            def _():
                to_right[b] = part[b].astype(BF16)

            right(b).start()

        @pl.when(t >= planes - 1 - z)
        def _():
            b = t - (planes - 1 - z)

            @pl.when(z < planes - 1)
            def _():
                left(b).wait_recv()
                to_left[b] = (part[b] + from_right[b].astype(F32)).astype(BF16)

            @pl.when(z == planes - 1)
            def _():
                to_left[b] = part[b].astype(BF16)

            left(b).start()

    @pl.when(z > 0)
    def _():
        right(z).wait_recv()
        part[z] += from_left[z].astype(F32)

    @pl.when(z < planes - 1)
    def _():
        left(z).wait_recv()
        part[z] += from_right[z].astype(F32)

    other = pl.ds(pl.multiple_of((1 - y) * share, 64), share)
    own = pl.ds(pl.multiple_of(y * share, 64), share)
    swap_out[...] = part[z, other, :].astype(BF16)
    swap = copy(swap_out, swap_in, xy_send.at[6], xy_recv.at[6], yn)
    swap.start()

    for tiny in gain_zs:
        tiny.wait_recv()
    total_gain = gain_sum[...]
    for step in range(planes - 1):
        total_gain = total_gain + gain_z[step]
    gain_out[...] = total_gain

    @pl.when(y == 0)
    def _():
        out_ref[:, :half] = part[z, own, :]

    @pl.when(y == 1)
    def _():
        out_ref[:, half:] = part[z, own, :]

    swap.wait_recv()

    @pl.when(y == 0)
    def _():
        out_ref[:, half:] = swap_in[...].astype(F32)

    @pl.when(y == 1)
    def _():
        out_ref[:, :half] = swap_in[...].astype(F32)

    for sent in [gain_x, act_x, up_y, up_x, act_y, act_d, up_d, gain_y, swap] + gain_zs:
        sent.wait_send()
    for t in range(planes - 1):
        @pl.when(t >= z)
        def _():
            right(planes - 1 - t + z).wait_send()

        @pl.when(t >= planes - 1 - z)
        def _():
            left(t - (planes - 1 - z)).wait_send()


def reduce_weight(act2, up2, gain):
    count = lax.axis_size("dp")
    planes = count // 4
    _, tokens, half = act2.shape
    rows = half // planes
    share = rows // 2
    vmem = pl.BlockSpec(memory_space=pltpu.VMEM)
    block = (planes, rows, half)
    sems = pltpu.SemaphoreType.DMA
    return pl.pallas_call(
        functools.partial(weight_kernel, planes),
        out_shape=(
            jax.ShapeDtypeStruct((share, 2 * half), F32),
            jax.ShapeDtypeStruct(gain.shape, F32),
        ),
        in_specs=[vmem] * 3,
        out_specs=(vmem, vmem),
        scratch_shapes=[
            pltpu.VMEM((3, tokens, half), BF16),
            pltpu.VMEM((3, tokens, half), BF16),
            pltpu.VMEM(block, F32),
            pltpu.VMEM(block, BF16),
            pltpu.VMEM(block, BF16),
            pltpu.VMEM(block, BF16),
            pltpu.VMEM(block, BF16),
            pltpu.VMEM((share, half), BF16),
            pltpu.VMEM((share, half), BF16),
            pltpu.VMEM((2,) + gain.shape, F32),
            pltpu.VMEM(gain.shape, F32),
            pltpu.VMEM(gain.shape, F32),
            pltpu.VMEM((planes - 1,) + gain.shape, F32),
            sems((7,)), sems((7,)), sems((planes,)), sems((planes,)),
            sems((planes,)), sems((planes,)), sems((planes + 1,)), sems((planes + 1,)),
        ],
        compiler_params=pltpu.CompilerParams(
            collective_id=0, has_side_effects=True, vmem_limit_bytes=40 << 20
        ),
    )(act2, up2, gain)


def body(section_inputs, mix_weight, norm_gain, out_cotangent, positions):
    sections = lax.axis_size("section")
    section_id = lax.axis_index("section")
    micro, tok_mb, channels = section_inputs.shape[1:]
    tokens = micro * tok_mb
    count = lax.axis_size("dp")
    planes = count // 4
    share = channels // count
    inputs = section_inputs[0].reshape(tokens, channels).astype(F32)
    cot = out_cotangent.reshape(tokens, channels)
    factor = 1.0 + 0.5 * jnp.sin(2.0 * math.pi * positions.reshape(tokens, 1).astype(F32) / DEPTH)
    weight_mat = mix_weight[0]
    gain_vec = norm_gain[0]
    inv_rms = lax.rsqrt(jnp.mean(inputs * inputs, axis=-1, keepdims=True) + 1e-06)
    normed = inputs * inv_rms * gain_vec
    activation, gelu_back = jax.vjp(jax.nn.gelu, normed)
    slope = gelu_back(jnp.ones_like(normed))[0]
    act2 = (
        activation.astype(BF16)
        .reshape(tokens, planes, 2, 2, share)
        .transpose(3, 0, 1, 2, 4)
        .reshape(2, tokens, channels // 2)
    )
    act2, slope, inv_rms, factor = lax.optimization_barrier((act2, slope, inv_rms, factor))

    grad_out = cot
    for step in range(sections):
        upstream = (factor * grad_out.astype(F32)).astype(BF16)
        back = lax.dot_general(
            upstream, weight_mat, (((1,), (1,)), ((), ())), preferred_element_type=F32
        )
        grad_norm = back * slope
        scaled = grad_norm * gain_vec
        projected = jnp.mean(scaled * inputs, axis=-1, keepdims=True)
        delta = inv_rms * scaled - inputs * (inv_rms * inv_rms * inv_rms) * projected
        grad_in = (grad_out.astype(F32) + delta).astype(BF16)
        if step < sections - 1:
            pairs = [(s, s - 1) for s in range(1, sections)]
            received = lax.ppermute(grad_in, "section", pairs)
            grad_out = jnp.where(section_id == sections - 1, cot, received)
    gain_term = jnp.sum(grad_norm * inputs * inv_rms, axis=0)[None]
    up2 = upstream.reshape(tokens, 2, channels // 2).transpose(1, 0, 2)
    weight_grad, gain_all = reduce_weight(act2, up2, gain_term)
    gain_share = lax.dynamic_slice_in_dim(gain_all[0], lax.axis_index("dp") * share, share, 0)
    return (grad_in.reshape(1, micro, tok_mb, channels), weight_grad[None], gain_share[None])


def solution(mesh):
    return jax.shard_map(
        body,
        mesh=mesh,
        in_specs=(
            P("section", None, "dp", None),
            P("section", None, None),
            P("section", None),
            P(None, "dp", None),
            P(None, "dp"),
        ),
        out_specs=(P("section", None, "dp", None), P("section", "dp", None), P("section", "dp")),
        check_vma=False,
    )
```

```python
import functools
import math

import jax
import jax.numpy as jnp
from jax import lax
from jax.experimental import pallas as pl
from jax.experimental.pallas import tpu as pltpu
from jax.sharding import PartitionSpec as P

DEPTH = 1024
MESH = pl.DeviceIdType.MESH
F32 = jnp.float32
BF16 = jnp.bfloat16


def outer_sum(a, b):
    return lax.dot_general(a, b, (((0,), (0,)), ((), ())), preferred_element_type=F32)


ROOT = math.sqrt(2.0 / math.pi)
CUBE = 0.044715


def back_kernel(
    planes, sections, x_hbm, w_hbm, cot_hbm, gain_ref, factor_ref, out_ref, gain_out, grads_ref,
    x_ref, w_ref, g_ref, slope, act_ref, up_ref, q_ref, m_ref, proj,
    gath_a, gath_u, part, from_left, from_right, to_right, to_left, swap_out, swap_in,
    gain_own, gain_in, gain_mid, gain_sum, gain_z,
    in_sem, sec_send, sec_recv,
    xy_send, xy_recv, r_send, r_recv, l_send, l_recv, g_send, g_recv,
):
    me = lax.axis_index("dp")
    sec = lax.axis_index("section")
    last = sections - 1
    total = planes * 4
    x = lax.rem(me, 2)
    y = lax.rem(me // 2, 2)
    z = me // 4
    xn = me + 1 - 2 * x
    yn = me + 2 - 4 * y
    tokens, channels = x_ref.shape
    half = channels // 2
    rows = half // planes
    share = rows // 2
    micro, tok_mb = factor_ref.shape
    step_rows = 16
    width = min(256, channels)

    load_x = pltpu.make_async_copy(x_hbm, x_ref, in_sem.at[0])
    load_w = pltpu.make_async_copy(w_hbm, w_ref, in_sem.at[1])
    load_g = pltpu.make_async_copy(cot_hbm, g_ref, in_sem.at[2])
    load_x.start()

    def copy(src, dst, send, recv, to):
        return pltpu.make_async_remote_copy(
            src_ref=src, dst_ref=dst, send_sem=send, recv_sem=recv,
            device_id={"dp": to}, device_id_type=MESH,
        )

    barrier = pltpu.get_barrier_semaphore()
    z_peers = [lax.rem(me + 4 * step, total) for step in range(1, planes)]
    for peer in [xn, yn] + z_peers:
        pl.semaphore_signal(barrier, inc=1, device_id={"dp": peer}, device_id_type=MESH)

    @pl.when(sec > 0)
    def _():
        pl.semaphore_signal(barrier, inc=1, device_id={"section": sec - 1}, device_id_type=MESH)

    @pl.when(sec < last)
    def _():
        pl.semaphore_signal(barrier, inc=1, device_id={"section": sec + 1}, device_id_type=MESH)

    @pl.when(sec == last)
    def _():
        load_g.start()

    load_w.start()

    for mb in range(micro):
        m_ref[mb * tok_mb:(mb + 1) * tok_mb, :] = jnp.transpose(
            jnp.broadcast_to(factor_ref[mb:mb + 1, :], (128, tok_mb))
        )
    proj[...] = jnp.zeros_like(proj)
    load_x.wait()

    @pl.loop(0, tokens // step_rows)
    def _(i):
        r = pl.ds(pl.multiple_of(i * step_rows, step_rows), step_rows)
        square = jnp.zeros((step_rows, rows), F32)
        for c in range(channels // rows):
            xc = x_ref[r, c * rows:(c + 1) * rows].astype(F32)
            square = square + xc * xc
        q = lax.rsqrt(jnp.sum(square, axis=-1, keepdims=True) / channels + 1e-06)
        q_ref[r, :] = jnp.broadcast_to(q, (step_rows, 128))
        for c in range(channels // rows):
            cols = slice(c * rows, (c + 1) * rows)
            n = x_ref[r, cols].astype(F32) * q * gain_ref[:, cols]
            n2 = n * n
            th = jnp.tanh(ROOT * (n + CUBE * (n2 * n)))
            cdf = 0.5 * (1.0 + th)
            act_ref[c % 2, r, (c // 2) * rows:(c // 2 + 1) * rows] = (n * cdf).astype(BF16)
            slope[r, cols] = cdf + (0.5 * ROOT) * n * (1.0 - th * th) * (1.0 + (3.0 * CUBE) * n2)

    beside = jnp.minimum(sec, 1) + jnp.minimum(last - sec, 1)
    pl.semaphore_wait(barrier, 1 + planes + beside)

    act_y = copy(act_ref.at[1 - y], gath_a.at[1], xy_send.at[0], xy_recv.at[0], yn)
    act_x = copy(act_ref.at[y], gath_a.at[0], xy_send.at[1], xy_recv.at[1], xn)
    up_x = copy(up_ref.at[1 - x], gath_u.at[0], xy_send.at[2], xy_recv.at[2], xn)
    up_y = copy(up_ref.at[x], gath_u.at[1], xy_send.at[3], xy_recv.at[3], yn)
    act_d = copy(gath_a.at[1], gath_a.at[2], xy_send.at[4], xy_recv.at[4], xn)
    up_d = copy(gath_u.at[0], gath_u.at[2], xy_send.at[5], xy_recv.at[5], yn)
    gain_x = copy(gain_own, gain_in.at[0], g_send.at[0], g_recv.at[0], xn)
    gain_y = copy(gain_mid, gain_in.at[1], g_send.at[1], g_recv.at[1], yn)
    act_y.start()
    act_x.start()

    def relay(mb):
        span = pl.ds(mb * tok_mb, tok_mb)
        return pltpu.make_async_remote_copy(
            src_ref=grads_ref.at[span, :], dst_ref=g_ref.at[span, :],
            send_sem=sec_send.at[mb], recv_sem=sec_recv.at[mb],
            device_id={"section": jnp.maximum(sec - 1, 0)}, device_id_type=MESH,
        )

    @pl.when(sec < last)
    def _():
        act_y.wait_recv()
        act_d.start()

    @pl.when(sec == last)
    def _():
        load_g.wait()

    for mb in range(micro):
        @pl.when(sec < last)
        def _():
            relay(mb).wait_recv()

        @pl.loop(mb * (tok_mb // step_rows), (mb + 1) * (tok_mb // step_rows))
        def _(i):
            r = pl.ds(pl.multiple_of(i * step_rows, step_rows), step_rows)
            m = m_ref[r, :1]
            for h in range(2):
                g = g_ref[r, h * half:(h + 1) * half].astype(F32)
                up_ref[h, r, :] = (m * g).astype(BF16)

    up_x.start()
    up_y.start()
    load_w.wait()

    @pl.loop(0, channels // width)
    def _(c):
        cols = pl.ds(pl.multiple_of(c * width, width), width)
        last_dims = (((1,), (1,)), ((), ()))
        back = lax.dot_general(
            up_ref[0], w_ref[cols, :half], last_dims, preferred_element_type=F32
        ) + lax.dot_general(up_ref[1], w_ref[cols, half:], last_dims, preferred_element_type=F32)
        grad_norm = back * slope[:, cols]
        xc = x_ref[:, cols].astype(F32)
        scaled = grad_norm * gain_ref[:, cols]
        slope[:, cols] = scaled
        along = scaled * xc
        lanes = proj[...]
        for k in range(width // 128):
            lanes = lanes + along[:, k * 128:(k + 1) * 128]
        proj[...] = lanes
        gain_own[:, cols] = jnp.sum(grad_norm * xc * q_ref[:, :1], axis=0, keepdims=True)

    for mb in range(micro):
        @pl.loop(mb * (tok_mb // step_rows), (mb + 1) * (tok_mb // step_rows))
        def _(i):
            r = pl.ds(pl.multiple_of(i * step_rows, step_rows), step_rows)
            q = q_ref[r, :1]
            pull = (q * q * q) * (jnp.sum(proj[r, :], axis=-1, keepdims=True) / channels)
            for c in range(channels // width):
                cols = slice(c * width, (c + 1) * width)
                delta = q * slope[r, cols] - x_ref[r, cols].astype(F32) * pull
                grads_ref[r, cols] = (g_ref[r, cols].astype(F32) + delta).astype(BF16)

        @pl.when(sec > 0)
        def _():
            relay(mb).start()

    @pl.when(sec == last)
    def _():
        act_y.wait_recv()
        act_d.start()

    up_x.wait_recv()
    up_d.start()
    gain_x.start()

    @pl.loop(0, planes)
    def _(b):
        cols = pl.ds(pl.multiple_of(b * rows, 128), rows)
        part[b] = outer_sum(act_ref[y, :, cols], up_ref[x])

    def add_source(slot):
        @pl.loop(0, planes)
        def _(b):
            cols = pl.ds(pl.multiple_of(b * rows, 128), rows)
            part[b] += outer_sum(gath_a[slot, :, cols], gath_u[slot])

    act_x.wait_recv()
    add_source(0)
    up_y.wait_recv()
    add_source(1)
    gain_x.wait_recv()
    gain_mid[...] = gain_own[...] + gain_in[0]
    gain_y.start()
    act_d.wait_recv()
    up_d.wait_recv()
    add_source(2)
    gain_y.wait_recv()
    gain_sum[...] = gain_mid[...] + gain_in[1]
    gain_zs = [
        copy(gain_sum, gain_z.at[step], g_send.at[2 + step], g_recv.at[2 + step], z_peers[step])
        for step in range(planes - 1)
    ]
    for tiny in gain_zs:
        tiny.start()

    z_next = lax.rem(me + 4, total)
    z_prev = lax.rem(me + total - 4, total)

    def right(b):
        return copy(to_right.at[b], from_left.at[b], r_send.at[b], r_recv.at[b], z_next)

    def left(b):
        return copy(to_left.at[b], from_right.at[b], l_send.at[b], l_recv.at[b], z_prev)

    for t in range(planes - 1):
        @pl.when(t >= z)
        def _():
            b = planes - 1 - t + z

            @pl.when(z > 0)
            def _():
                right(b).wait_recv()
                to_right[b] = (part[b] + from_left[b].astype(F32)).astype(BF16)

            @pl.when(z == 0)
            def _():
                to_right[b] = part[b].astype(BF16)

            right(b).start()

        @pl.when(t >= planes - 1 - z)
        def _():
            b = t - (planes - 1 - z)

            @pl.when(z < planes - 1)
            def _():
                left(b).wait_recv()
                to_left[b] = (part[b] + from_right[b].astype(F32)).astype(BF16)

            @pl.when(z == planes - 1)
            def _():
                to_left[b] = part[b].astype(BF16)

            left(b).start()

    @pl.when(z > 0)
    def _():
        right(z).wait_recv()
        part[z] += from_left[z].astype(F32)

    @pl.when(z < planes - 1)
    def _():
        left(z).wait_recv()
        part[z] += from_right[z].astype(F32)

    other = pl.ds(pl.multiple_of((1 - x) * share, 64), share)
    own = pl.ds(pl.multiple_of(x * share, 64), share)
    swap_out[...] = part[z, other, :].astype(BF16)
    swap = copy(swap_out, swap_in, xy_send.at[6], xy_recv.at[6], xn)
    swap.start()

    for tiny in gain_zs:
        tiny.wait_recv()
    total_gain = gain_sum[...]
    for step in range(planes - 1):
        total_gain = total_gain + gain_z[step]
    gain_out[...] = total_gain

    @pl.when(x == 0)
    def _():
        out_ref[:, :half] = part[z, own, :]

    @pl.when(x == 1)
    def _():
        out_ref[:, half:] = part[z, own, :]

    swap.wait_recv()

    @pl.when(x == 0)
    def _():
        out_ref[:, half:] = swap_in[...].astype(F32)

    @pl.when(x == 1)
    def _():
        out_ref[:, :half] = swap_in[...].astype(F32)

    for sent in [gain_x, act_x, up_y, up_x, act_y, act_d, up_d, gain_y, swap] + gain_zs:
        sent.wait_send()
    for t in range(planes - 1):
        @pl.when(t >= z)
        def _():
            right(planes - 1 - t + z).wait_send()

        @pl.when(t >= planes - 1 - z)
        def _():
            left(t - (planes - 1 - z)).wait_send()

    @pl.when(sec > 0)
    def _():
        for mb in range(micro):
            relay(mb).wait_send()


def body(section_inputs, mix_weight, norm_gain, out_cotangent, positions):
    sections = lax.axis_size("section")
    micro, tok_mb, channels = section_inputs.shape[1:]
    tokens = micro * tok_mb
    count = lax.axis_size("dp")
    planes = count // 4
    share = channels // count
    half = channels // 2
    rows = half // planes
    factor = 1.0 + 0.5 * jnp.sin(2.0 * math.pi * positions.astype(F32) / DEPTH)
    vmem = pl.BlockSpec(memory_space=pltpu.VMEM)
    hbm = pl.BlockSpec(memory_space=pl.ANY)
    block = (planes, rows, half)
    line = (1, channels)
    sems = pltpu.SemaphoreType.DMA
    weight_grad, gain_all, grads = pl.pallas_call(
        functools.partial(back_kernel, planes, sections),
        out_shape=(
            jax.ShapeDtypeStruct((share, channels), F32),
            jax.ShapeDtypeStruct(line, F32),
            jax.ShapeDtypeStruct((tokens, channels), BF16),
        ),
        in_specs=[hbm, hbm, hbm, vmem, vmem],
        out_specs=(vmem, vmem, vmem),
        scratch_shapes=[
            pltpu.VMEM((tokens, channels), BF16),
            pltpu.VMEM((channels, channels), BF16),
            pltpu.VMEM((tokens, channels), BF16),
            pltpu.VMEM((tokens, channels), F32),
            pltpu.VMEM((2, tokens, half), BF16),
            pltpu.VMEM((2, tokens, half), BF16),
            pltpu.VMEM((tokens, 128), F32),
            pltpu.VMEM((tokens, 128), F32),
            pltpu.VMEM((tokens, 128), F32),
            pltpu.VMEM((3, tokens, half), BF16),
            pltpu.VMEM((3, tokens, half), BF16),
            pltpu.VMEM(block, F32),
            pltpu.VMEM(block, BF16),
            pltpu.VMEM(block, BF16),
            pltpu.VMEM(block, BF16),
            pltpu.VMEM(block, BF16),
            pltpu.VMEM((share, half), BF16),
            pltpu.VMEM((share, half), BF16),
            pltpu.VMEM(line, F32),
            pltpu.VMEM((2,) + line, F32),
            pltpu.VMEM(line, F32),
            pltpu.VMEM(line, F32),
            pltpu.VMEM((planes - 1,) + line, F32),
            sems((3,)), sems((micro,)), sems((micro,)),
            sems((7,)), sems((7,)), sems((planes,)), sems((planes,)),
            sems((planes,)), sems((planes,)), sems((planes + 1,)), sems((planes + 1,)),
        ],
        compiler_params=pltpu.CompilerParams(
            collective_id=0, has_side_effects=True, vmem_limit_bytes=56 << 20
        ),
    )(
        section_inputs.reshape(tokens, channels),
        mix_weight[0],
        out_cotangent.reshape(tokens, channels),
        norm_gain,
        factor,
    )
    gain_share = lax.dynamic_slice_in_dim(gain_all[0], lax.axis_index("dp") * share, share, 0)
    return (grads.reshape(1, micro, tok_mb, channels), weight_grad[None], gain_share[None])


def solution(mesh):
    return jax.shard_map(
        body,
        mesh=mesh,
        in_specs=(
            P("section", None, "dp", None),
            P("section", None, None),
            P("section", None),
            P(None, "dp", None),
            P(None, "dp"),
        ),
        out_specs=(P("section", None, "dp", None), P("section", "dp", None), P("section", "dp")),
        check_vma=False,
    )
```

```python
import functools
import math

import jax
import jax.numpy as jnp
from jax import lax
from jax.experimental import pallas as pl
from jax.experimental.pallas import tpu as pltpu
from jax.sharding import PartitionSpec as P

DEPTH = 1024
MESH = pl.DeviceIdType.MESH
F32 = jnp.float32
BF16 = jnp.bfloat16


def outer_sum(a, b):
    return lax.dot_general(a, b, (((0,), (0,)), ((), ())), preferred_element_type=F32)


ROOT = math.sqrt(2.0 / math.pi)
CUBE = 0.044715
CHUNKS = 2


def back_kernel(
    planes, sections, x_hbm, w_hbm, cot_hbm, gain_ref, factor_ref, out_ref, gain_out, grads_ref,
    x_ref, w_ref, g_ref, slope, act_ref, up_ref, q_ref, m_ref, proj,
    gath_a, gath_u, part, from_left, from_right, to_right, to_left, swap_out, swap_in,
    gain_own, gain_in, gain_mid, gain_sum, gain_z,
    in_sem, sec_send, sec_recv, u_send, u_recv, s_send, s_recv,
    xy_send, xy_recv, r_send, r_recv, l_send, l_recv, g_send, g_recv,
):
    me = lax.axis_index("dp")
    sec = lax.axis_index("section")
    last = sections - 1
    total = planes * 4
    x = lax.rem(me, 2)
    y = lax.rem(me // 2, 2)
    z = me // 4
    xn = me + 1 - 2 * x
    yn = me + 2 - 4 * y
    tokens, channels = x_ref.shape
    half = channels // 2
    rows = half // planes
    share = rows // 2
    micro, tok_mb = factor_ref.shape
    step_rows = 16
    width = min(256, channels)
    part_cols = half // CHUNKS

    load_x = pltpu.make_async_copy(x_hbm, x_ref, in_sem.at[0])
    load_w = pltpu.make_async_copy(w_hbm, w_ref, in_sem.at[1])
    load_g = pltpu.make_async_copy(cot_hbm, g_ref, in_sem.at[2])
    load_x.start()

    def copy(src, dst, send, recv, to):
        return pltpu.make_async_remote_copy(
            src_ref=src, dst_ref=dst, send_sem=send, recv_sem=recv,
            device_id={"dp": to}, device_id_type=MESH,
        )

    barrier = pltpu.get_barrier_semaphore()
    z_peers = [lax.rem(me + 4 * step, total) for step in range(1, planes)]
    for peer in [xn, yn] + z_peers:
        pl.semaphore_signal(barrier, inc=1, device_id={"dp": peer}, device_id_type=MESH)

    @pl.when(sec > 0)
    def _():
        pl.semaphore_signal(barrier, inc=1, device_id={"section": sec - 1}, device_id_type=MESH)

    @pl.when(sec < last)
    def _():
        pl.semaphore_signal(barrier, inc=1, device_id={"section": sec + 1}, device_id_type=MESH)

    @pl.when(sec == last)
    def _():
        load_g.start()

    load_w.start()

    for mb in range(micro):
        m_ref[mb * tok_mb:(mb + 1) * tok_mb, :] = jnp.transpose(
            jnp.broadcast_to(factor_ref[mb:mb + 1, :], (128, tok_mb))
        )
    proj[...] = jnp.zeros_like(proj)
    load_x.wait()

    @pl.loop(0, tokens // step_rows)
    def _(i):
        r = pl.ds(pl.multiple_of(i * step_rows, step_rows), step_rows)
        square = jnp.zeros((step_rows, rows), F32)
        for c in range(channels // rows):
            xc = x_ref[r, c * rows:(c + 1) * rows].astype(F32)
            square = square + xc * xc
        q = lax.rsqrt(jnp.sum(square, axis=-1, keepdims=True) / channels + 1e-06)
        q_ref[r, :] = jnp.broadcast_to(q, (step_rows, 128))
        for c in range(channels // rows):
            cols = slice(c * rows, (c + 1) * rows)
            n = x_ref[r, cols].astype(F32) * q * gain_ref[:, cols]
            n2 = n * n
            th = jnp.tanh(ROOT * (n + CUBE * (n2 * n)))
            cdf = 0.5 * (1.0 + th)
            act_ref[c % 2, r, (c // 2) * rows:(c // 2 + 1) * rows] = (n * cdf).astype(BF16)
            slope[r, cols] = cdf + (0.5 * ROOT) * n * (1.0 - th * th) * (1.0 + (3.0 * CUBE) * n2)

    beside = jnp.minimum(sec, 1) + jnp.minimum(last - sec, 1)
    pl.semaphore_wait(barrier, 1 + planes + beside)

    act_y = copy(act_ref.at[1 - y], gath_a.at[1], xy_send.at[0], xy_recv.at[0], yn)
    act_x = copy(act_ref.at[y], gath_a.at[0], xy_send.at[1], xy_recv.at[1], xn)
    up_x = [
        copy(up_ref.at[(1 - x) * CHUNKS + k], gath_u.at[k], u_send.at[k], u_recv.at[k], xn)
        for k in range(CHUNKS)
    ]
    up_y = [
        copy(
            up_ref.at[x * CHUNKS + k], gath_u.at[CHUNKS + k],
            u_send.at[CHUNKS + k], u_recv.at[CHUNKS + k], yn,
        )
        for k in range(CHUNKS)
    ]
    up_d = [
        copy(
            gath_u.at[k], gath_u.at[2 * CHUNKS + k],
            u_send.at[2 * CHUNKS + k], u_recv.at[2 * CHUNKS + k], yn,
        )
        for k in range(CHUNKS)
    ]
    act_d = copy(gath_a.at[1], gath_a.at[2], xy_send.at[4], xy_recv.at[4], xn)
    gain_x = copy(gain_own, gain_in.at[0], g_send.at[0], g_recv.at[0], xn)
    gain_y = copy(gain_mid, gain_in.at[1], g_send.at[1], g_recv.at[1], yn)
    def relay(mb):
        span = pl.ds(mb * tok_mb, tok_mb)
        return pltpu.make_async_remote_copy(
            src_ref=grads_ref.at[span, :], dst_ref=g_ref.at[span, :],
            send_sem=sec_send.at[mb], recv_sem=sec_recv.at[mb],
            device_id={"section": jnp.maximum(sec - 1, 0)}, device_id_type=MESH,
        )

    @pl.when(sec < last)
    def _():
        relay(0).wait_recv()

    act_y.start()
    act_x.start()

    @pl.when(sec == last)
    def _():
        load_g.wait()

    for mb in range(micro):
        if mb > 0:
            @pl.when(sec < last)
            def _():
                relay(mb).wait_recv()

        @pl.loop(mb * (tok_mb // step_rows), (mb + 1) * (tok_mb // step_rows))
        def _(i):
            r = pl.ds(pl.multiple_of(i * step_rows, step_rows), step_rows)
            m = m_ref[r, :1]
            for h in range(2 * CHUNKS):
                g = g_ref[r, h * part_cols:(h + 1) * part_cols].astype(F32)
                up_ref[h, r, :] = (m * g).astype(BF16)

    up_x[0].start()
    up_y[0].start()
    load_w.wait()

    @pl.loop(0, channels // width)
    def _(c):
        cols = pl.ds(pl.multiple_of(c * width, width), width)
        last_dims = (((1,), (1,)), ((), ()))
        back = jnp.zeros((tokens, width), F32)
        for h in range(2 * CHUNKS):
            back = back + lax.dot_general(
                up_ref[h], w_ref[cols, h * part_cols:(h + 1) * part_cols], last_dims,
                preferred_element_type=F32,
            )
        grad_norm = back * slope[:, cols]
        xc = x_ref[:, cols].astype(F32)
        scaled = grad_norm * gain_ref[:, cols]
        slope[:, cols] = scaled
        along = scaled * xc
        lanes = proj[...]
        for k in range(width // 128):
            lanes = lanes + along[:, k * 128:(k + 1) * 128]
        proj[...] = lanes
        gain_own[:, cols] = jnp.sum(grad_norm * xc * q_ref[:, :1], axis=0, keepdims=True)

    for mb in range(micro):
        @pl.loop(mb * (tok_mb // step_rows), (mb + 1) * (tok_mb // step_rows))
        def _(i):
            r = pl.ds(pl.multiple_of(i * step_rows, step_rows), step_rows)
            q = q_ref[r, :1]
            pull = (q * q * q) * (jnp.sum(proj[r, :], axis=-1, keepdims=True) / channels)
            for c in range(channels // width):
                cols = slice(c * width, (c + 1) * width)
                delta = q * slope[r, cols] - x_ref[r, cols].astype(F32) * pull
                grads_ref[r, cols] = (g_ref[r, cols].astype(F32) + delta).astype(BF16)

        @pl.when(sec > 0)
        def _():
            relay(mb).start()

    act_y.wait_recv()
    act_d.start()
    up_x[0].wait_recv()
    up_d[0].start()
    gain_x.start()
    for k in range(1, CHUNKS):
        up_x[k].start()
        up_y[k].start()

    for k in range(CHUNKS):
        @pl.loop(0, planes)
        def _(b):
            cols = pl.ds(pl.multiple_of(b * rows, 128), rows)
            part[k * planes + b] = outer_sum(act_ref[y, :, cols], up_ref[x * CHUNKS + k])

    def add_source(slot, k):
        @pl.loop(0, planes)
        def _(b):
            cols = pl.ds(pl.multiple_of(b * rows, 128), rows)
            part[k * planes + b] += outer_sum(gath_a[slot, :, cols], gath_u[slot * CHUNKS + k])

    z_next = lax.rem(me + 4, total)
    z_prev = lax.rem(me + total - 4, total)

    def right(at):
        return copy(to_right.at[at], from_left.at[at], r_send.at[at], r_recv.at[at], z_next)

    def left(at):
        return copy(to_left.at[at], from_right.at[at], l_send.at[at], l_recv.at[at], z_prev)

    def z_step(t, k):
        @pl.when(t >= z)
        def _():
            at = k * planes + planes - 1 - t + z

            @pl.when(z > 0)
            def _():
                right(at).wait_recv()
                to_right[at] = (part[at] + from_left[at].astype(F32)).astype(BF16)

            @pl.when(z == 0)
            def _():
                to_right[at] = part[at].astype(BF16)

            right(at).start()

        @pl.when(t >= planes - 1 - z)
        def _():
            at = k * planes + t - (planes - 1 - z)

            @pl.when(z < planes - 1)
            def _():
                left(at).wait_recv()
                to_left[at] = (part[at] + from_right[at].astype(F32)).astype(BF16)

            @pl.when(z == planes - 1)
            def _():
                to_left[at] = part[at].astype(BF16)

            left(at).start()

    act_x.wait_recv()
    for k in range(CHUNKS):
        if k == 0:
            add_source(0, 0)
        up_y[k].wait_recv()
        add_source(1, k)
        if k == 0:
            act_d.wait_recv()
        up_d[k].wait_recv()
        add_source(2, k)
        z_step(0, k)
        if k + 1 < CHUNKS:
            up_x[k + 1].wait_recv()
            up_d[k + 1].start()
        for t in range(1, planes - 1):
            z_step(t, k)
        if k + 1 < CHUNKS:
            add_source(0, k + 1)

    gain_x.wait_recv()
    gain_mid[...] = gain_own[...] + gain_in[0]
    gain_y.start()
    other = pl.ds(pl.multiple_of((1 - x) * share, 64), share)
    own = pl.ds(pl.multiple_of(x * share, 64), share)
    swaps = [
        copy(swap_out.at[k], swap_in.at[k], s_send.at[k], s_recv.at[k], xn)
        for k in range(CHUNKS)
    ]

    def finish(k):
        at = k * planes + z

        @pl.when(z > 0)
        def _():
            right(at).wait_recv()
            part[at] += from_left[at].astype(F32)

        @pl.when(z < planes - 1)
        def _():
            left(at).wait_recv()
            part[at] += from_right[at].astype(F32)

        swap_out[k] = part[at, other, :].astype(BF16)
        swaps[k].start()
        for side in range(2):
            @pl.when(x == side)
            def _():
                lo = side * half + k * part_cols
                out_ref[:, lo:lo + part_cols] = part[at, own, :]

    for k in range(CHUNKS - 1):
        finish(k)
    gain_y.wait_recv()
    gain_sum[...] = gain_mid[...] + gain_in[1]
    gain_zs = [
        copy(gain_sum, gain_z.at[step], g_send.at[2 + step], g_recv.at[2 + step], z_peers[step])
        for step in range(planes - 1)
    ]
    for tiny in gain_zs:
        tiny.start()

    finish(CHUNKS - 1)
    for tiny in gain_zs:
        tiny.wait_recv()
    total_gain = gain_sum[...]
    for step in range(planes - 1):
        total_gain = total_gain + gain_z[step]
    gain_out[...] = total_gain

    for k in range(CHUNKS):
        swaps[k].wait_recv()
        for side in range(2):
            @pl.when(x == side)
            def _():
                lo = (1 - side) * half + k * part_cols
                out_ref[:, lo:lo + part_cols] = swap_in[k].astype(F32)

    for sent in [act_x, act_y, act_d, gain_x, gain_y] + up_x + up_y + up_d + swaps + gain_zs:
        sent.wait_send()
    for k in range(CHUNKS):
        for t in range(planes - 1):
            @pl.when(t >= z)
            def _():
                right(k * planes + planes - 1 - t + z).wait_send()

            @pl.when(t >= planes - 1 - z)
            def _():
                left(k * planes + t - (planes - 1 - z)).wait_send()

    @pl.when(sec > 0)
    def _():
        for mb in range(micro):
            relay(mb).wait_send()


def body(section_inputs, mix_weight, norm_gain, out_cotangent, positions):
    sections = lax.axis_size("section")
    micro, tok_mb, channels = section_inputs.shape[1:]
    tokens = micro * tok_mb
    count = lax.axis_size("dp")
    planes = count // 4
    share = channels // count
    half = channels // 2
    rows = half // planes
    factor = 1.0 + 0.5 * jnp.sin(2.0 * math.pi * positions.astype(F32) / DEPTH)
    vmem = pl.BlockSpec(memory_space=pltpu.VMEM)
    hbm = pl.BlockSpec(memory_space=pltpu.HBM)
    part_cols = half // CHUNKS
    hops = CHUNKS * planes
    block = (hops, rows, part_cols)
    line = (1, channels)
    sems = pltpu.SemaphoreType.DMA
    weight_grad, gain_all, grads = pl.pallas_call(
        functools.partial(back_kernel, planes, sections),
        out_shape=(
            jax.ShapeDtypeStruct((share, channels), F32),
            jax.ShapeDtypeStruct(line, F32),
            jax.ShapeDtypeStruct((tokens, channels), BF16),
        ),
        in_specs=[hbm, hbm, hbm, vmem, vmem],
        out_specs=(vmem, vmem, vmem),
        scratch_shapes=[
            pltpu.VMEM((tokens, channels), BF16),
            pltpu.VMEM((channels, channels), BF16),
            pltpu.VMEM((tokens, channels), BF16),
            pltpu.VMEM((tokens, channels), F32),
            pltpu.VMEM((2, tokens, half), BF16),
            pltpu.VMEM((2 * CHUNKS, tokens, part_cols), BF16),
            pltpu.VMEM((tokens, 128), F32),
            pltpu.VMEM((tokens, 128), F32),
            pltpu.VMEM((tokens, 128), F32),
            pltpu.VMEM((3, tokens, half), BF16),
            pltpu.VMEM((3 * CHUNKS, tokens, part_cols), BF16),
            pltpu.VMEM(block, F32),
            pltpu.VMEM(block, BF16),
            pltpu.VMEM(block, BF16),
            pltpu.VMEM(block, BF16),
            pltpu.VMEM(block, BF16),
            pltpu.VMEM((CHUNKS, share, part_cols), BF16),
            pltpu.VMEM((CHUNKS, share, part_cols), BF16),
            pltpu.VMEM(line, F32),
            pltpu.VMEM((2,) + line, F32),
            pltpu.VMEM(line, F32),
            pltpu.VMEM(line, F32),
            pltpu.VMEM((planes - 1,) + line, F32),
            sems((3,)), sems((micro,)), sems((micro,)),
            sems((3 * CHUNKS,)), sems((3 * CHUNKS,)), sems((CHUNKS,)), sems((CHUNKS,)),
            sems((5,)), sems((5,)), sems((hops,)), sems((hops,)),
            sems((hops,)), sems((hops,)), sems((planes + 1,)), sems((planes + 1,)),
        ],
        compiler_params=pltpu.CompilerParams(
            collective_id=0, has_side_effects=True, vmem_limit_bytes=53 << 20
        ),
    )(
        section_inputs.reshape(tokens, channels),
        mix_weight[0],
        out_cotangent.reshape(tokens, channels),
        norm_gain,
        factor,
    )
    gain_share = lax.dynamic_slice_in_dim(gain_all[0], lax.axis_index("dp") * share, share, 0)
    return (grads.reshape(1, micro, tok_mb, channels), weight_grad[None], gain_share[None])


def solution(mesh):
    return jax.shard_map(
        body,
        mesh=mesh,
        in_specs=(
            P("section", None, "dp", None),
            P("section", None, None),
            P("section", None),
            P(None, "dp", None),
            P(None, "dp"),
        ),
        out_specs=(P("section", None, "dp", None), P("section", "dp", None), P("section", "dp")),
        check_vma=False,
    )
```

```python
import functools
import math

import jax
import jax.numpy as jnp
from jax import lax
from jax.experimental import pallas as pl
from jax.experimental.pallas import tpu as pltpu
from jax.sharding import PartitionSpec as P

DEPTH = 1024
MESH = pl.DeviceIdType.MESH
F32 = jnp.float32
BF16 = jnp.bfloat16


def outer_sum(a, b):
    return lax.dot_general(a, b, (((0,), (0,)), ((), ())), preferred_element_type=F32)


ROOT = math.sqrt(2.0 / math.pi)
CUBE = 0.044715
CHUNKS = 2


def back_kernel(
    planes, sections, x_hbm, w_hbm, cot_hbm, gain_ref, factor_ref, out_ref, gain_out, grads_ref,
    x_ref, w_ref, g_ref, slope, act_ref, up_ref, q_ref, m_ref, proj,
    gath_a, gath_u, part, from_left, from_right, to_right, to_left, swap_out, swap_in,
    gain_own, gain_in, gain_mid, gain_sum, gain_z,
    in_sem, sec_send, sec_recv, u_send, u_recv, s_send, s_recv,
    xy_send, xy_recv, r_send, r_recv, l_send, l_recv, g_send, g_recv,
):
    me = lax.axis_index("dp")
    sec = lax.axis_index("section")
    last = sections - 1
    total = planes * 4
    x = lax.rem(me, 2)
    y = lax.rem(me // 2, 2)
    z = me // 4
    xn = me + 1 - 2 * x
    yn = me + 2 - 4 * y
    tokens, channels = x_ref.shape
    half = channels // 2
    rows = half // planes
    share = rows // 2
    micro, tok_mb = factor_ref.shape
    step_rows = 16
    width = min(256, channels)
    part_cols = half // CHUNKS

    load_x = pltpu.make_async_copy(x_hbm, x_ref, in_sem.at[0])
    load_w = pltpu.make_async_copy(w_hbm, w_ref, in_sem.at[1])
    load_g = pltpu.make_async_copy(cot_hbm, g_ref, in_sem.at[2])
    load_x.start()

    def copy(src, dst, send, recv, to):
        return pltpu.make_async_remote_copy(
            src_ref=src, dst_ref=dst, send_sem=send, recv_sem=recv,
            device_id={"dp": to}, device_id_type=MESH,
        )

    barrier = pltpu.get_barrier_semaphore()
    z_peers = [lax.rem(me + 4 * step, total) for step in range(1, planes)]
    for peer in [xn, yn] + z_peers:
        pl.semaphore_signal(barrier, inc=1, device_id={"dp": peer}, device_id_type=MESH)

    @pl.when(sec > 0)
    def _():
        pl.semaphore_signal(barrier, inc=1, device_id={"section": sec - 1}, device_id_type=MESH)

    @pl.when(sec < last)
    def _():
        pl.semaphore_signal(barrier, inc=1, device_id={"section": sec + 1}, device_id_type=MESH)

    @pl.when(sec == last)
    def _():
        load_g.start()

    load_w.start()

    for mb in range(micro):
        m_ref[mb * tok_mb:(mb + 1) * tok_mb, :] = jnp.transpose(
            jnp.broadcast_to(factor_ref[mb:mb + 1, :], (128, tok_mb))
        )
    proj[...] = jnp.zeros_like(proj)
    load_x.wait()

    @pl.loop(0, tokens // step_rows)
    def _(i):
        r = pl.ds(pl.multiple_of(i * step_rows, step_rows), step_rows)
        square = jnp.zeros((step_rows, rows), F32)
        for c in range(channels // rows):
            xc = x_ref[r, c * rows:(c + 1) * rows].astype(F32)
            square = square + xc * xc
        q = lax.rsqrt(jnp.sum(square, axis=-1, keepdims=True) / channels + 1e-06)
        q_ref[r, :] = jnp.broadcast_to(q, (step_rows, 128))
        for c in range(channels // rows):
            cols = slice(c * rows, (c + 1) * rows)
            n = x_ref[r, cols].astype(F32) * q * gain_ref[:, cols]
            n2 = n * n
            th = jnp.tanh(ROOT * (n + CUBE * (n2 * n)))
            cdf = 0.5 * (1.0 + th)
            act_ref[c % 2, r, (c // 2) * rows:(c // 2 + 1) * rows] = (n * cdf).astype(BF16)
            slope[r, cols] = cdf + (0.5 * ROOT) * n * (1.0 - th * th) * (1.0 + (3.0 * CUBE) * n2)

    beside = jnp.minimum(sec, 1) + jnp.minimum(last - sec, 1)
    pl.semaphore_wait(barrier, 1 + planes + beside)

    act_y = copy(act_ref.at[1 - y], gath_a.at[1], xy_send.at[0], xy_recv.at[0], yn)
    act_x = copy(act_ref.at[y], gath_a.at[0], xy_send.at[1], xy_recv.at[1], xn)
    up_x = [
        copy(up_ref.at[(1 - x) * CHUNKS + k], gath_u.at[k], u_send.at[k], u_recv.at[k], xn)
        for k in range(CHUNKS)
    ]
    up_y = [
        copy(
            up_ref.at[x * CHUNKS + k], gath_u.at[CHUNKS + k],
            u_send.at[CHUNKS + k], u_recv.at[CHUNKS + k], yn,
        )
        for k in range(CHUNKS)
    ]
    up_d = [
        copy(
            gath_u.at[k], gath_u.at[2 * CHUNKS + k],
            u_send.at[2 * CHUNKS + k], u_recv.at[2 * CHUNKS + k], yn,
        )
        for k in range(CHUNKS)
    ]
    act_d = copy(gath_a.at[1], gath_a.at[2], xy_send.at[4], xy_recv.at[4], xn)
    gain_x = copy(gain_own, gain_in.at[0], g_send.at[0], g_recv.at[0], xn)
    gain_y = copy(gain_mid, gain_in.at[1], g_send.at[1], g_recv.at[1], yn)
    def relay(mb):
        span = pl.ds(mb * tok_mb, tok_mb)
        return pltpu.make_async_remote_copy(
            src_ref=grads_ref.at[span, :], dst_ref=g_ref.at[span, :],
            send_sem=sec_send.at[mb], recv_sem=sec_recv.at[mb],
            device_id={"section": jnp.maximum(sec - 1, 0)}, device_id_type=MESH,
        )

    @pl.when(sec < last)
    def _():
        relay(0).wait_recv()

    act_y.start()
    act_x.start()

    @pl.when(sec == last)
    def _():
        load_g.wait()

    for mb in range(micro):
        if mb > 0:
            @pl.when(sec < last)
            def _():
                relay(mb).wait_recv()

        @pl.loop(mb * (tok_mb // step_rows), (mb + 1) * (tok_mb // step_rows))
        def _(i):
            r = pl.ds(pl.multiple_of(i * step_rows, step_rows), step_rows)
            m = m_ref[r, :1]
            for h in range(2 * CHUNKS):
                g = g_ref[r, h * part_cols:(h + 1) * part_cols].astype(F32)
                up_ref[h, r, :] = (m * g).astype(BF16)

    up_x[0].start()
    up_y[0].start()
    load_w.wait()

    @pl.loop(0, channels // width)
    def _(c):
        cols = pl.ds(pl.multiple_of(c * width, width), width)
        last_dims = (((1,), (1,)), ((), ()))
        back = jnp.zeros((tokens, width), F32)
        for h in range(2 * CHUNKS):
            back = back + lax.dot_general(
                up_ref[h], w_ref[cols, h * part_cols:(h + 1) * part_cols], last_dims,
                preferred_element_type=F32,
            )
        grad_norm = back * slope[:, cols]
        xc = x_ref[:, cols].astype(F32)
        scaled = grad_norm * gain_ref[:, cols]
        slope[:, cols] = scaled
        along = scaled * xc
        lanes = proj[...]
        for k in range(width // 128):
            lanes = lanes + along[:, k * 128:(k + 1) * 128]
        proj[...] = lanes
        gain_own[:, cols] = jnp.sum(grad_norm * xc * q_ref[:, :1], axis=0, keepdims=True)

    for mb in range(micro):
        @pl.loop(mb * (tok_mb // step_rows), (mb + 1) * (tok_mb // step_rows))
        def _(i):
            r = pl.ds(pl.multiple_of(i * step_rows, step_rows), step_rows)
            q = q_ref[r, :1]
            pull = (q * q * q) * (jnp.sum(proj[r, :], axis=-1, keepdims=True) / channels)
            for c in range(channels // width):
                cols = slice(c * width, (c + 1) * width)
                delta = q * slope[r, cols] - x_ref[r, cols].astype(F32) * pull
                grads_ref[r, cols] = (g_ref[r, cols].astype(F32) + delta).astype(BF16)

        @pl.when(sec > 0)
        def _():
            relay(mb).start()

    act_y.wait_recv()
    act_d.start()
    up_x[0].wait_recv()
    up_d[0].start()
    gain_x.start()
    for k in range(1, CHUNKS):
        up_x[k].start()
        up_y[k].start()

    for k in range(CHUNKS):
        @pl.loop(0, planes)
        def _(b):
            cols = pl.ds(pl.multiple_of(b * rows, 128), rows)
            part[k * planes + b] = outer_sum(act_ref[y, :, cols], up_ref[x * CHUNKS + k])

    def add_source(slot, k):
        @pl.loop(0, planes)
        def _(b):
            cols = pl.ds(pl.multiple_of(b * rows, 128), rows)
            part[k * planes + b] += outer_sum(gath_a[slot, :, cols], gath_u[slot * CHUNKS + k])

    z_next = lax.rem(me + 4, total)
    z_prev = lax.rem(me + total - 4, total)

    def right(at):
        return copy(to_right.at[at], from_left.at[at], r_send.at[at], r_recv.at[at], z_next)

    def left(at):
        return copy(to_left.at[at], from_right.at[at], l_send.at[at], l_recv.at[at], z_prev)

    def z_step(t, k):
        @pl.when(t >= z)
        def _():
            at = k * planes + planes - 1 - t + z

            @pl.when(z > 0)
            def _():
                right(at).wait_recv()
                to_right[at] = (part[at] + from_left[at].astype(F32)).astype(BF16)

            @pl.when(z == 0)
            def _():
                to_right[at] = part[at].astype(BF16)

            right(at).start()

        @pl.when(t >= planes - 1 - z)
        def _():
            at = k * planes + t - (planes - 1 - z)

            @pl.when(z < planes - 1)
            def _():
                left(at).wait_recv()
                to_left[at] = (part[at] + from_right[at].astype(F32)).astype(BF16)

            @pl.when(z == planes - 1)
            def _():
                to_left[at] = part[at].astype(BF16)

            left(at).start()

    act_x.wait_recv()
    for k in range(CHUNKS):
        if k == 0:
            add_source(0, 0)
        up_y[k].wait_recv()
        add_source(1, k)
        if k == 0:
            act_d.wait_recv()
        up_d[k].wait_recv()
        add_source(2, k)
        z_step(0, k)
        if k + 1 < CHUNKS:
            up_x[k + 1].wait_recv()
            up_d[k + 1].start()
        for t in range(1, planes - 1):
            z_step(t, k)
        if k + 1 < CHUNKS:
            add_source(0, k + 1)

    gain_x.wait_recv()
    gain_mid[...] = gain_own[...] + gain_in[0]
    gain_y.start()
    other = pl.ds(pl.multiple_of((1 - x) * share, 64), share)
    own = pl.ds(pl.multiple_of(x * share, 64), share)
    swaps = [
        copy(swap_out.at[k], swap_in.at[k], s_send.at[k], s_recv.at[k], xn)
        for k in range(CHUNKS)
    ]

    def finish(k):
        at = k * planes + z

        @pl.when(z > 0)
        def _():
            right(at).wait_recv()
            part[at] += from_left[at].astype(F32)

        @pl.when(z < planes - 1)
        def _():
            left(at).wait_recv()
            part[at] += from_right[at].astype(F32)

        swap_out[k] = part[at, other, :].astype(BF16)
        swaps[k].start()
        for side in range(2):
            @pl.when(x == side)
            def _():
                lo = side * half + k * part_cols
                out_ref[:, lo:lo + part_cols] = part[at, own, :]

    for k in range(CHUNKS - 1):
        finish(k)
    gain_y.wait_recv()
    gain_sum[...] = gain_mid[...] + gain_in[1]
    gain_zs = [
        copy(gain_sum, gain_z.at[step], g_send.at[2 + step], g_recv.at[2 + step], z_peers[step])
        for step in range(planes - 1)
    ]
    for tiny in gain_zs:
        tiny.start()

    finish(CHUNKS - 1)
    for tiny in gain_zs:
        tiny.wait_recv()
    total_gain = gain_sum[...]
    for step in range(planes - 1):
        total_gain = total_gain + gain_z[step]
    gain_out[...] = total_gain

    for k in range(CHUNKS):
        swaps[k].wait_recv()
        for side in range(2):
            @pl.when(x == side)
            def _():
                lo = (1 - side) * half + k * part_cols
                out_ref[:, lo:lo + part_cols] = swap_in[k].astype(F32)

    for sent in [act_x, act_y, act_d, gain_x, gain_y] + up_x + up_y + up_d + swaps + gain_zs:
        sent.wait_send()
    for k in range(CHUNKS):
        for t in range(planes - 1):
            @pl.when(t >= z)
            def _():
                right(k * planes + planes - 1 - t + z).wait_send()

            @pl.when(t >= planes - 1 - z)
            def _():
                left(k * planes + t - (planes - 1 - z)).wait_send()

    @pl.when(sec > 0)
    def _():
        for mb in range(micro):
            relay(mb).wait_send()


def body(section_inputs, mix_weight, norm_gain, out_cotangent, positions):
    sections = lax.axis_size("section")
    micro, tok_mb, channels = section_inputs.shape[1:]
    tokens = micro * tok_mb
    count = lax.axis_size("dp")
    planes = count // 4
    share = channels // count
    half = channels // 2
    rows = half // planes
    factor = 1.0 + 0.5 * jnp.sin(2.0 * math.pi * positions.astype(F32) / DEPTH)
    vmem = pl.BlockSpec(memory_space=pltpu.VMEM)
    hbm = pl.BlockSpec(memory_space=pltpu.HBM)
    part_cols = half // CHUNKS
    hops = CHUNKS * planes
    block = (hops, rows, part_cols)
    line = (1, channels)
    sems = pltpu.SemaphoreType.DMA
    weight_grad, gain_all, grads = pl.pallas_call(
        functools.partial(back_kernel, planes, sections),
        out_shape=(
            jax.ShapeDtypeStruct((share, channels), F32),
            jax.ShapeDtypeStruct(line, F32),
            jax.ShapeDtypeStruct((tokens, channels), BF16),
        ),
        in_specs=[hbm, hbm, hbm, vmem, vmem],
        out_specs=(vmem, vmem, vmem),
        scratch_shapes=[
            pltpu.VMEM((tokens, channels), BF16),
            pltpu.VMEM((channels, channels), BF16),
            pltpu.VMEM((tokens, channels), BF16),
            pltpu.VMEM((tokens, channels), F32),
            pltpu.VMEM((2, tokens, half), BF16),
            pltpu.VMEM((2 * CHUNKS, tokens, part_cols), BF16),
            pltpu.VMEM((tokens, 128), F32),
            pltpu.VMEM((tokens, 128), F32),
            pltpu.VMEM((tokens, 128), F32),
            pltpu.VMEM((3, tokens, half), BF16),
            pltpu.VMEM((3 * CHUNKS, tokens, part_cols), BF16),
            pltpu.VMEM(block, F32),
            pltpu.VMEM(block, BF16),
            pltpu.VMEM(block, BF16),
            pltpu.VMEM(block, BF16),
            pltpu.VMEM(block, BF16),
            pltpu.VMEM((CHUNKS, share, part_cols), BF16),
            pltpu.VMEM((CHUNKS, share, part_cols), BF16),
            pltpu.VMEM(line, F32),
            pltpu.VMEM((2,) + line, F32),
            pltpu.VMEM(line, F32),
            pltpu.VMEM(line, F32),
            pltpu.VMEM((planes - 1,) + line, F32),
            sems((3,)), sems((micro,)), sems((micro,)),
            sems((3 * CHUNKS,)), sems((3 * CHUNKS,)), sems((CHUNKS,)), sems((CHUNKS,)),
            sems((5,)), sems((5,)), sems((hops,)), sems((hops,)),
            sems((hops,)), sems((hops,)), sems((planes + 1,)), sems((planes + 1,)),
        ],
        compiler_params=pltpu.CompilerParams(
            collective_id=0, has_side_effects=True, vmem_limit_bytes=50 << 20
        ),
    )(
        section_inputs.reshape(tokens, channels),
        mix_weight[0],
        out_cotangent.reshape(tokens, channels),
        norm_gain,
        factor,
    )
    gain_share = lax.dynamic_slice_in_dim(gain_all[0], lax.axis_index("dp") * share, share, 0)
    return (grads.reshape(1, micro, tok_mb, channels), weight_grad[None], gain_share[None])


def solution(mesh):
    return jax.shard_map(
        body,
        mesh=mesh,
        in_specs=(
            P("section", None, "dp", None),
            P("section", None, None),
            P("section", None),
            P(None, "dp", None),
            P(None, "dp"),
        ),
        out_specs=(P("section", None, "dp", None), P("section", "dp", None), P("section", "dp")),
        check_vma=False,
    )
```
